32 devices in a mesh: groups: 2 (over x), arc: 2 (over core), blk: 8 (over z, y).
Axes of the slice: x: 2, y: 2, z: 4, core: 2. Of those that a mesh axis runs over, the one named last changes fastest.
Arguments:
- queries: bfloat16 [6144, 640], P(('groups', 'arc', 'blk')), parts along dimension 0, may hold values from -128 to 128
- keys: bfloat16 [6144, 640], P(('groups', 'arc', 'blk')), parts along dimension 0, may hold values from -4 to 4
- values: bfloat16 [6144, 640], P(('groups', 'arc', 'blk')), parts along dimension 0, may hold values from -6 to 6
- out_weight: bfloat16 [640, 1024], replicated, may hold values from -0.25 to 0.25
- covis: int32 [192, 96], P('groups'), parts along dimension 0, may hold values from 0 to 1, as said below
- block_view: int32 [192], P('groups'), parts along dimension 0, may hold values from 0 to 95, each once
Outputs:
- projected: bfloat16 [6144, 1024], P(('groups', 'arc', 'blk')), parts along dimension 0
The draws below stay inside these ranges and needn't reach their ends.
There are 2 independent parts, one for each index of `groups`. The reference program is written for one: setup_inputs(seed, part) draws one part's arguments, and reference() takes and returns one part's arrays. A program takes and returns all parts, laid end to end along the dimension named above; an argument that names none is the same for every part. Nothing has to cross between parts.
Inputs may be any that keep to these rules, and one draw needn't show every extreme that they name: `covis`: symmetric, with ones on the diagonal. `block_view`: each view once.
All inputs are finite; a program needn't handle non-finite values.
Results may differ from the reference program's by a relative error of at most 0.008.
Values may be sent and summed in bfloat16 or wider, within the bound.
No kernel may reach another device: no remote copies, remote signals or barrier semaphores. Data moves between devices by JAX's collectives and lax.ppermute only.
A program may use at most 128 MiB of HBM per device.

```python
import jax
import jax.numpy as jnp
from jax import lax

D = 1024
HEADS = 10
HD = 64
BLOCK = 32
TOKENS = 3072
NB = 96


def make_pair(key):
    base = jax.random.fold_in(key, 101)
    key_q, key_k = jax.random.split(base, 2)
    width = HEADS * HD
    query_part = jax.random.truncated_normal(key_q, -4.0, 4.0, (TOKENS, width), jnp.float32)
    key_part = jax.random.truncated_normal(key_k, -4.0, 4.0, (TOKENS, width), jnp.float32)
    query_part = 2.0 * query_part
    return (query_part, key_part)


def draw_queries(key, part):
    return make_pair(key)[0].astype(jnp.bfloat16)


def draw_keys(key, part):
    return make_pair(key)[1].astype(jnp.bfloat16)


def draw_covis(key, part):
    base = jax.random.fold_in(key, 202)
    key_a, key_b = jax.random.split(base, 2)
    raw = jax.random.randint(key_a, (NB, NB), 0, 16)
    paired = raw + raw.T
    index = jnp.arange(NB, dtype=jnp.int32)
    apart = jnp.abs(index[:, None] - index[None, :])
    apart = jnp.minimum(apart, NB - apart)
    reach = jax.random.randint(key_b, (NB,), 1, NB // 2 + 1)
    limit = jnp.maximum(reach[:, None], reach[None, :])
    linked = (apart <= limit) & (paired >= 8)
    linked = linked | (index[:, None] == index[None, :])
    return linked.astype(jnp.int32)


def block_scale(key, extent, cuts, low, high):
    def one(position, parts):
        steps = jax.random.uniform(jax.random.fold_in(jax.random.fold_in(key, 6), position), (parts,), jnp.float32, low / len(cuts), high / len(cuts))
        return jnp.repeat(jnp.exp(steps), extent[position] // parts).reshape((-1,) + (1,) * (len(extent) - position - 1))

    gain = one(*cuts[0])
    for cut in cuts[1:]:
        gain = gain * one(*cut)
    return gain


def scatter_about(own_key, extent, deviation, most, shards=(), kind=jnp.bfloat16):
    factor_of = block_scale(own_key, extent, shards, -0.22, 0.18) if shards else 1.0
    entries = jax.random.normal(own_key, extent, jnp.float32) * deviation * factor_of
    return jnp.minimum(jnp.maximum(entries, -most), most).astype(kind)


def setup_inputs(seed: int = 0, part: int = 0) -> dict:
    splits = jax.random.split(jax.random.key(seed), 7)
    own_keys = jax.random.split(jax.random.fold_in(splits[6], part), 7)
    return {
        "queries": draw_queries(jax.random.fold_in(jax.random.fold_in(splits[6], part), 71), part),
        "keys": draw_keys(jax.random.fold_in(jax.random.fold_in(splits[6], part), 71), part),
        "values": scatter_about(own_keys[2], (TOKENS, HEADS * HD), 1.0, 6.0, ((0, 16),)),
        "out_weight": scatter_about(splits[3], (HEADS * HD, D), (HEADS * HD) ** -0.5, 0.25),
        "covis": draw_covis(jax.random.fold_in(jax.random.fold_in(splits[6], part), 71), part),
        "block_view": jax.random.permutation(own_keys[5], NB).astype(jnp.int32),
    }


NEG = -1e30


def reference(queries, keys, values, out_weight, covis, block_view):
    vis = covis[block_view][:, block_view]
    scale = HD ** -0.5
    k3 = keys.astype(jnp.float32).reshape(TOKENS, HEADS, HD)
    v3 = values.astype(jnp.float32).reshape(TOKENS, HEADS, HD)
    q4 = queries.reshape(NB, BLOCK, HEADS, HD)

    def one_block(index):
        q = lax.dynamic_index_in_dim(q4, index, 0, keepdims=False).astype(jnp.float32)
        row = lax.dynamic_index_in_dim(vis, index, 0, keepdims=False)
        keep = (jnp.repeat(row, BLOCK) > 0)[None, None, :]
        scores = jnp.einsum("qhd,khd->qhk", q, k3) * scale
        scores = jnp.where(keep, scores, NEG)
        peak = jnp.max(scores, axis=-1, keepdims=True)
        probs = jnp.where(keep, jnp.exp(scores - peak), 0.0)
        total = jnp.sum(probs, axis=-1)
        rounded = lax.optimization_barrier(probs.astype(jnp.bfloat16))
        mixed = jnp.einsum("qhk,khd->qhd", rounded.astype(jnp.float32), v3) / total[..., None]
        return mixed.reshape(BLOCK, HEADS * HD).astype(jnp.bfloat16)

    attn = lax.map(one_block, jnp.arange(NB, dtype=jnp.int32)).reshape(TOKENS, HEADS * HD)
    return jnp.dot(attn, out_weight, preferred_element_type=jnp.float32).astype(jnp.bfloat16)
```

```python
import functools

import jax
import jax.numpy as jnp
from jax import lax
from jax.experimental import pallas as pl
from jax.experimental.pallas import tpu as pltpu
from jax.sharding import PartitionSpec as P

HEADS = 10
HD = 64
BLOCK = 32
BIG = 1e30
PAIRS = HEADS // 2
GROUPS = ((0, 3), (3, 5))
LANES = 128
WIDE = 256
AHEAD = 3
SLOTS = 16
F32 = jnp.float32
BF16 = jnp.bfloat16
LIMIT = 24 << 20


def steps_of(n):
    rest = list(range(1, n // 2))
    return [(0,)] + [tuple(rest[i : i + 2]) for i in range(0, len(rest), 2)]


def query_blocks(tok):
    per = tok // BLOCK
    cut = tok // LANES * LANES // BLOCK
    return [(0, j) for j in range(per)] + [(1, j) for j in range(cut, per)] + [(1, j) for j in range(cut)]


def key_marks(keys):
    place = lax.broadcasted_iota(jnp.int32, (keys, LANES), 0) // BLOCK
    lane = lax.broadcasted_iota(jnp.int32, (keys, LANES), 1)
    return (place == lane).astype(F32).astype(BF16)


def run_tiles(pieces, base, qbd_ref, rows, state_in, state_out, pairs):
    acc_in, ml_in = state_in
    acc_out, ml_out = state_out
    tok = pieces[0].shape[0] // 2
    parts = len(pieces)
    wide = qbd_ref.shape[2]
    marks = key_marks(parts * tok)
    pad = jnp.zeros((LANES - SLOTS, WIDE), BF16)
    items = [(p - pairs[0], p, t) for p in range(*pairs) for t in range(wide // WIDE)]
    turned = {}
    ones = jnp.ones((16, parts * tok), BF16)

    def joined(p, row):
        cols = slice((p - base) * 2 * HD, (p - base + 1) * 2 * HD)
        got = [ref[row : row + tok, cols] for ref in pieces]
        return got[0] if parts == 1 else jnp.concatenate(got, axis=0)

    def score(item):
        _, p, t = item
        lanes = slice(t * WIDE, (t + 1) * WIDE)
        lhs = jnp.concatenate([joined(p, 0), marks], axis=1)
        rhs = jnp.concatenate([qbd_ref[p, :, lanes], rows[:, lanes], pad], axis=0)
        return jnp.dot(lhs, rhs, preferred_element_type=F32)

    def soft(item, scores):
        at, p, t = item
        lanes = slice(t * WIDE, (t + 1) * WIDE)
        top = jnp.max(scores, axis=0, keepdims=True)
        old = None
        if ml_in is not None:
            old = ml_in[at : at + 1, lanes]
            top = jnp.maximum(old, top)
        probs = jnp.exp(scores - top)
        if p not in turned:
            turned[p] = jnp.concatenate([joined(p, tok).T, ones], axis=0)
        mixed = jnp.dot(turned[p], probs.astype(BF16), preferred_element_type=F32)
        return old, top, mixed

    def store(item, old, top, mixed):
        at, _, t = item
        lanes = slice(t * WIDE, (t + 1) * WIDE)
        total = mixed[2 * HD : 2 * HD + 1, :]
        mixed = jnp.concatenate([mixed[:HD, :LANES], mixed[HD : 2 * HD, LANES:]], axis=1)
        if old is not None:
            factor = jnp.exp(old - top)
            total = total + factor * ml_in[8 + at : 9 + at, lanes]
            mixed = mixed + factor * acc_in[at, :, lanes]
        acc_out[at, :, lanes] = mixed
        ml_out[at : at + 1, lanes] = top
        ml_out[8 + at : 9 + at, lanes] = total

    ready = [score(item) for item in items[:AHEAD]]
    waiting = None
    for i, item in enumerate(items):
        if i + AHEAD < len(items):
            ready.append(score(items[i + AHEAD]))
        now = soft(item, ready.pop(0))
        if waiting is not None:
            store(*waiting)
        waiting = (item, *now)
    store(*waiting)


def first_kernel(views_ref, q_ref, qo_ref, *refs, n_blk, across):
    n_groups = len(GROUPS)
    kv_refs = refs[:n_groups]
    qbd_ref, rows_ref = refs[n_groups : n_groups + 2]
    states = refs[n_groups + 2 : 3 * n_groups + 2]
    bv_ref, pick_ref, sem = refs[3 * n_groups + 2 :]
    tok = qo_ref.shape[0]
    count = views_ref.shape[1]
    move = pltpu.make_async_copy(views_ref.at[count : count + 1, :], bv_ref, sem)
    move.start()
    per = tok // BLOCK
    cut = tok // LANES * LANES
    chunks = 2 * tok // LANES
    arc = lax.axis_index("arc")
    blk = lax.axis_index("blk")
    move.wait()
    lane = lax.broadcasted_iota(jnp.int32, (1, 2 * tok), 1) // BLOCK
    view = jnp.zeros((1, 2 * tok), jnp.int32)
    for at, (half, j) in enumerate(query_blocks(tok)):
        base = ((arc if half == 0 else 1 - arc) * n_blk + jnp.bitwise_xor(blk, across)) * per
        view = jnp.where(lane == at, bv_ref[0, base + j], view)
    sub = lax.broadcasted_iota(jnp.int32, (count, 2 * tok), 0)
    pick = (sub == view).astype(F32).astype(BF16)
    pick_ref[...] = jnp.zeros_like(pick_ref)
    seen = lax.broadcasted_iota(jnp.int32, (1, count), 1)
    for step, far in enumerate(steps_of(n_blk)):
        for i, d in enumerate(far):
            base = (arc * n_blk + jnp.bitwise_xor(blk, d)) * per
            for j in range(per):
                at = step * SLOTS + i * per + j
                pick_ref[at : at + 1, :] = (seen == bv_ref[0, base + j]).astype(F32)
    scale = jnp.asarray(HD ** -0.5, BF16)
    qt = (jnp.concatenate([q_ref[...], qo_ref[cut:, :], qo_ref[:cut, :]], axis=0) * scale).T
    zero = jnp.zeros((HD, LANES), BF16)
    for p in range(PAIRS):
        for c in range(chunks):
            a = qt[p * 2 * HD : p * 2 * HD + HD, c * LANES : (c + 1) * LANES]
            b = qt[p * 2 * HD + HD : (p + 1) * 2 * HD, c * LANES : (c + 1) * LANES]
            left = slice(c * 2 * LANES, c * 2 * LANES + LANES)
            right = slice(c * 2 * LANES + LANES, (c + 1) * 2 * LANES)
            qbd_ref[p, :HD, left] = a
            qbd_ref[p, :HD, right] = zero
            qbd_ref[p, HD:, left] = zero
            qbd_ref[p, HD:, right] = b
    table = views_ref[:count, :].astype(F32).astype(BF16)
    qvis = jnp.dot(table, pick, preferred_element_type=F32).astype(BF16)
    keep = jnp.dot(pick_ref[...].astype(BF16), qvis, preferred_element_type=F32)
    bias = ((keep - 1.0) * BIG).astype(BF16)
    for c in range(chunks):
        part = bias[:, c * LANES : (c + 1) * LANES]
        rows_ref[:, c * 2 * LANES : c * 2 * LANES + LANES] = part
        rows_ref[:, c * 2 * LANES + LANES : (c + 1) * 2 * LANES] = part
    for g, pairs in enumerate(GROUPS):
        acc_ref, ml_ref = states[2 * g : 2 * g + 2]
        ml_ref[...] = jnp.zeros_like(ml_ref)
        run_tiles(
            (kv_refs[g],), pairs[0], qbd_ref, rows_ref[:SLOTS, :], (None, None), (acc_ref, ml_ref), pairs
        )


def write_packed(out_ref, acc, ml, n):
    low = lax.broadcasted_iota(jnp.int32, (HD, LANES), 1) < HD

    def packed(x, rows):
        side = jnp.where(low[:rows], x[:, 2 * LANES : 3 * LANES], pltpu.roll(x[:, 3 * LANES :], HD, 1))
        return jnp.concatenate([x[:, : 2 * LANES], side], axis=1)

    for p in range(n):
        out_ref[p * HD : (p + 1) * HD, :] = packed(acc(p), HD).astype(BF16)
    rest = packed(ml, 16)
    for i in range(3):
        part = rest.astype(BF16)
        out_ref[n * HD + 16 * i : n * HD + 16 * (i + 1), :] = part
        rest = rest - part.astype(F32)


def read_packed(ref, n):
    def spread(x):
        return jnp.concatenate([x, pltpu.roll(x[:, 2 * LANES :], HD, 1)], axis=1)

    acc = [spread(ref[p * HD : (p + 1) * HD, :].astype(F32)) for p in range(n)]
    ml = sum(ref[n * HD + 16 * i : n * HD + 16 * (i + 1), :].astype(F32) for i in range(3))
    return acc, spread(ml)


def block_kernel(*refs, step, pieces, pairs, last):
    qbd_ref, rows_ref, acc_in, ml_in = refs[:4]
    kv_refs = refs[4 : 4 + pieces]
    acc_ref, ml_ref = refs[4 + pieces : 6 + pieces]
    rows = rows_ref[step * SLOTS : (step + 1) * SLOTS, :]
    ml_ref[...] = jnp.zeros_like(ml_ref)
    run_tiles(kv_refs, pairs[0], qbd_ref, rows, (acc_in, ml_in), (acc_ref, ml_ref), pairs)
    if last:
        def theirs(x):
            a = pltpu.roll(x[:, 2 * LANES : 3 * LANES], HD, 1)
            b = pltpu.roll(x[:, 3 * LANES : 4 * LANES], HD, 1)
            return jnp.concatenate([x[:, 4 * LANES :], a, b], axis=1)

        n = pairs[1] - pairs[0]
        write_packed(refs[6 + pieces], lambda p: theirs(acc_ref[p]), theirs(ml_ref[...]), n)


def merged(n, states):
    out = []
    for p in range(n):
        tops = [ml[p : p + 1, :] for _, ml in states]
        top = functools.reduce(jnp.maximum, tops)
        factors = [jnp.exp(t - top) for t in tops]
        total = sum(f * ml[8 + p : 9 + p, :] for f, (_, ml) in zip(factors, states))
        out.append((top, total, factors))
    return out


def own_state(acc_ref, ml_ref, n):
    return [acc_ref[p, :, : 4 * LANES] for p in range(n)], ml_ref[:, : 4 * LANES]


def combine_kernel(acc_ref, ml_ref, got_ref, out_ref):
    n = acc_ref.shape[0]
    states = [own_state(acc_ref, ml_ref, n), read_packed(got_ref, n)]
    ml, accs = [], []
    table = merged(n, states)
    for p, (top, total, factors) in enumerate(table):
        accs.append(sum(f * acc[p] for f, (acc, _) in zip(factors, states)))
    zero = jnp.zeros((8 - n, 4 * LANES), F32)
    ml = [top for top, _, _ in table] + [zero] + [total for _, total, _ in table] + [zero]
    write_packed(out_ref, lambda p: accs[p], jnp.concatenate(ml, axis=0), n)


def finish_kernel(w_ref, *refs):
    out_ref = refs[-1]
    tok = out_ref.shape[0]
    parts = []
    for g, (lo, hi) in enumerate(GROUPS):
        acc_ref, ml_ref, got_ref, far_ref = refs[4 * g : 4 * g + 4]
        n = hi - lo
        states = [own_state(acc_ref, ml_ref, n), read_packed(got_ref, n), read_packed(far_ref, n)]
        for p, (top, total, factors) in enumerate(merged(n, states)):
            share = 1.0 / total
            mixed = sum((f * share) * acc[p] for f, (acc, _) in zip(factors, states))
            for i in range(2):
                first = mixed[:, i * LANES : (i + 1) * LANES]
                second = mixed[:, (2 + i) * LANES : (3 + i) * LANES]
                parts.append(jnp.concatenate([first, second], axis=1).astype(BF16))
    attn = jnp.concatenate(parts, axis=0).T[:tok]
    out_ref[...] = jnp.dot(attn, w_ref[...], preferred_element_type=F32).astype(BF16)


def vmem():
    return pl.BlockSpec(memory_space=pltpu.VMEM)


def hop(x, axis, flip):
    pairs = [(i, i ^ flip) for i in range(lax.axis_size(axis))]
    return lax.ppermute(x, axis, pairs)


def body(queries, keys, values, out_weight, covis, block_view):
    tok, _ = queries.shape
    count = covis.shape[0]
    n_blk = lax.axis_size("blk")
    half = n_blk // 2
    steps = steps_of(n_blk)
    last_step = len(steps) - 1
    shape = jax.ShapeDtypeStruct
    params = pltpu.CompilerParams(vmem_limit_bytes=LIMIT)
    sizes = [hi - lo for lo, hi in GROUPS]

    def cost(keys_seen, heads):
        return pl.CostEstimate(
            flops=8 * tok * keys_seen * HD * heads,
            bytes_accessed=2 << 20,
            transcendentals=2 * tok * keys_seen * heads,
        )

    own = []
    for lo, hi in GROUPS:
        cols = slice(lo * 2 * HD, hi * 2 * HD)
        own.append(jnp.concatenate([keys[:, cols], values[:, cols]], axis=0))
    views = jnp.concatenate([covis, block_view[None]], axis=0)
    blocks = [{0: x} for x in own]
    for g in range(len(GROUPS)):
        for d in range(1, half):
            low = d & -d
            if g % 2 and d != low:
                low = 1 << (d.bit_length() - 1)
            blocks[g][d] = hop(blocks[g][d ^ low], "blk", low)
    q_own = hop(queries, "arc", 1)
    q_far = hop(queries, "blk", half)
    q_far_own = hop(q_far, "arc", 1)

    def first(q, qo, across):
        states = [x for n in sizes for x in (shape((n, HD, 4 * tok), F32), shape((16, 4 * tok), F32))]
        return pl.pallas_call(
            functools.partial(first_kernel, n_blk=n_blk, across=across),
            out_shape=(
                shape((PAIRS, 2 * HD, 4 * tok), BF16),
                shape((len(steps) * SLOTS, 4 * tok), BF16),
                *states,
            ),
            in_specs=[vmem()] * (3 + len(own)),
            out_specs=(vmem(),) * (2 + len(states)),
            scratch_shapes=[
                pltpu.SMEM((1, count), jnp.int32),
                pltpu.VMEM((len(steps) * SLOTS, count), F32),
                pltpu.SemaphoreType.DMA,
            ],
            cost_estimate=cost(tok, HEADS),
            compiler_params=params,
            name="attend_first",
        )(views, q, qo, *own)

    near = first(queries, q_own, 0)
    far = first(q_far, q_far_own, half)

    def attend(setup, state, g, step):
        n = sizes[g]
        last = step == last_step
        pieces = [blocks[g][d] for d in steps[step]]
        outs = [shape((n, HD, 4 * tok), F32), shape((16, 4 * tok), F32)]
        if last:
            outs.append(shape((n * HD + 3 * 16, 2 * tok), BF16))
        operands = [*setup[:2], *state, *pieces]
        return pl.pallas_call(
            functools.partial(
                block_kernel, step=step, pieces=len(pieces), pairs=GROUPS[g], last=last
            ),
            out_shape=tuple(outs),
            in_specs=[vmem()] * len(operands),
            out_specs=tuple(vmem() for _ in outs),
            cost_estimate=cost(tok * len(pieces), 2 * n),
            compiler_params=params,
            name="attend",
        )(*operands)

    finals = []
    for g, n in enumerate(sizes):
        state = far[2 + 2 * g : 4 + 2 * g]
        for step in range(1, last_step + 1):
            state = attend(far, state[:2], g, step)
        acc, ml, send = state
        got = hop(send, "arc", 1)
        total = pl.pallas_call(
            combine_kernel,
            out_shape=shape(send.shape, BF16),
            in_specs=[vmem()] * 3,
            out_specs=vmem(),
            cost_estimate=pl.CostEstimate(flops=1 << 20, bytes_accessed=1 << 20, transcendentals=0),
            compiler_params=params,
            name="combine",
        )(acc, ml, got)
        home = hop(total, "blk", half)
        state = near[2 + 2 * g : 4 + 2 * g]
        for step in range(1, last_step + 1):
            state = attend(near, state[:2], g, step)
        acc, ml, send = state
        got = hop(send, "arc", 1)
        finals += [acc, ml, got, home]
    return pl.pallas_call(
        finish_kernel,
        out_shape=shape((tok, out_weight.shape[1]), BF16),
        in_specs=[vmem()] * (1 + len(finals)),
        out_specs=vmem(),
        compiler_params=params,
        name="finish",
    )(out_weight, *finals)


def solution(mesh):
    return jax.shard_map(
        body,
        mesh=mesh,
        in_specs=(
            P(("groups", "arc", "blk"), None),
            P(("groups", "arc", "blk"), None),
            P(("groups", "arc", "blk"), None),
            P(),
            P("groups", None),
            P("groups"),
        ),
        out_specs=P(("groups", "arc", "blk"), None),
        check_vma=False,
    )
```

```python
import functools

import jax
import jax.numpy as jnp
from jax import lax
from jax.experimental import pallas as pl
from jax.experimental.pallas import tpu as pltpu
from jax.sharding import PartitionSpec as P

HEADS = 10
HD = 64
BLOCK = 32
BIG = 1e30
PAIRS = HEADS // 2
LANES = 128
WIDE = 256
AHEAD = 3
ONES = True
SLOTS = 16
CHUNK = 256
OWN = 512
F32 = jnp.float32
BF16 = jnp.bfloat16
LIMIT = 24 << 20


def ring_order(n):
    if n == 8:
        return [0, 2, 4, 6, 7, 5, 3, 1]
    return list(range(n))


def ring_at(n, place):
    if n == 8:
        return jnp.where(place < 4, 2 * place, 2 * (7 - place) + 1)
    return place


def ring_place(n, blk):
    if n == 8:
        return jnp.where(blk % 2 == 0, blk // 2, 7 - blk // 2)
    return blk


def hops_of(step, n):
    if step == 0:
        return (0,)
    return (step,) if 2 * step == n else (step, n - step)


def query_blocks(tok):
    per = tok // BLOCK
    cut = tok // LANES * LANES // BLOCK
    return [(0, j) for j in range(per)] + [(1, j) for j in range(cut, per)] + [(1, j) for j in range(cut)]


def key_marks(keys):
    place = lax.broadcasted_iota(jnp.int32, (keys, LANES), 0) // BLOCK
    lane = lax.broadcasted_iota(jnp.int32, (keys, LANES), 1)
    return (place == lane).astype(F32).astype(BF16)


def run_tiles(pieces, qbd_ref, rows, state_in, state_out, pairs):
    acc_in, ml_in = state_in
    acc_out, ml_out = state_out
    tok = pieces[0].shape[0]
    parts = len(pieces) // 2
    wide = qbd_ref.shape[2]
    marks = key_marks(parts * tok)
    pad = jnp.zeros((LANES - SLOTS, WIDE), BF16)
    items = [(at, p, t) for at, p in enumerate(range(*pairs)) for t in range(wide // WIDE)]

    turned = {}
    ones = jnp.ones((16, parts * tok), BF16)

    def joined(refs, p):
        got = [ref[:, p * 2 * HD : (p + 1) * 2 * HD] for ref in refs]
        return got[0] if parts == 1 else jnp.concatenate(got, axis=0)

    def score(item):
        _, p, t = item
        lanes = slice(t * WIDE, (t + 1) * WIDE)
        lhs = jnp.concatenate([joined(pieces[0::2], p), marks], axis=1)
        rhs = jnp.concatenate([qbd_ref[p, :, lanes], rows[:, lanes], pad], axis=0)
        return jnp.dot(lhs, rhs, preferred_element_type=F32)

    def soft(item, scores):
        _, p, t = item
        lanes = slice(t * WIDE, (t + 1) * WIDE)
        top = jnp.max(scores, axis=0, keepdims=True)
        old = None
        if ml_in is not None:
            old = ml_in[p : p + 1, lanes]
            top = jnp.maximum(old, top)
        probs = jnp.exp(scores - top)
        total = None if ONES else jnp.sum(probs, axis=0, keepdims=True)
        if p not in turned:
            turned[p] = joined(pieces[1::2], p).T
            if ONES:
                turned[p] = jnp.concatenate([turned[p], ones], axis=0)
        vt = turned[p]
        mixed = jnp.dot(vt, probs.astype(BF16), preferred_element_type=F32)
        return old, top, total, mixed

    def store(item, old, top, total, mixed):
        at, p, t = item
        lanes = slice(t * WIDE, (t + 1) * WIDE)
        if ONES:
            total = mixed[2 * HD : 2 * HD + 1, :]
        cut = [
            mixed[HD * (i % 2) : HD * (i % 2) + HD, i * LANES : (i + 1) * LANES]
            for i in range(WIDE // LANES)
        ]
        mixed = jnp.concatenate(cut, axis=1)
        if old is not None:
            factor = jnp.exp(old - top)
            total = total + factor * ml_in[8 + p : 9 + p, lanes]
            mixed = mixed + factor * acc_in[p, :, lanes]
        acc_out[at, :, lanes] = mixed
        ml_out[at : at + 1, lanes] = top
        ml_out[8 + at : 9 + at, lanes] = total

    ready = [score(item) for item in items[:AHEAD]]
    waiting = None
    for i, item in enumerate(items):
        if i + AHEAD < len(items):
            ready.append(score(items[i + AHEAD]))
        now = soft(item, ready.pop(0))
        if waiting is not None:
            store(*waiting)
        waiting = (item, *now)
    store(*waiting)


def first_kernel(
    views_ref, qkv_ref, qo_ref, qbd_ref, rows_ref, acc_ref, ml_ref, bv_ref, pick_ref, sem, *, n_blk
):
    tok = qo_ref.shape[0]
    count = views_ref.shape[1]
    q_ref, k_ref, v_ref = (qkv_ref.at[i * tok : (i + 1) * tok] for i in range(3))
    move = pltpu.make_async_copy(views_ref.at[count : count + 1, :], bv_ref, sem)
    move.start()
    per = tok // BLOCK
    cut = tok // LANES * LANES
    chunks = 2 * tok // LANES
    arc = lax.axis_index("arc")
    blk = lax.axis_index("blk")
    place = ring_place(n_blk, blk)
    move.wait()
    lane = lax.broadcasted_iota(jnp.int32, (1, 2 * tok), 1) // BLOCK
    view = jnp.zeros((1, 2 * tok), jnp.int32)
    for at, (half, j) in enumerate(query_blocks(tok)):
        base = ((arc if half == 0 else 1 - arc) * n_blk + blk) * per
        view = jnp.where(lane == at, bv_ref[0, base + j], view)
    sub = lax.broadcasted_iota(jnp.int32, (count, 2 * tok), 0)
    pick = (sub == view).astype(F32).astype(BF16)
    pick_ref[...] = jnp.zeros_like(pick_ref)
    seen = lax.broadcasted_iota(jnp.int32, (1, count), 1)
    for step in range(n_blk // 2 + 1):
        blocks = [(hop, arc) for hop in hops_of(step, n_blk)]
        if 2 * step == n_blk:
            blocks.append((step, 1 - arc))
        for i, (hop, side) in enumerate(blocks):
            base = (side * n_blk + ring_at(n_blk, lax.rem(place + n_blk - hop, n_blk))) * per
            for j in range(per):
                at = step * SLOTS + i * per + j
                pick_ref[at : at + 1, :] = (seen == bv_ref[0, base + j]).astype(F32)
    scale = jnp.asarray(HD ** -0.5, BF16)
    qt = (jnp.concatenate([q_ref[...], qo_ref[cut:, :], qo_ref[:cut, :]], axis=0) * scale).T
    zero = jnp.zeros((HD, LANES), BF16)
    for p in range(PAIRS):
        for c in range(chunks):
            a = qt[p * 2 * HD : p * 2 * HD + HD, c * LANES : (c + 1) * LANES]
            b = qt[p * 2 * HD + HD : (p + 1) * 2 * HD, c * LANES : (c + 1) * LANES]
            left = slice(c * 2 * LANES, c * 2 * LANES + LANES)
            right = slice(c * 2 * LANES + LANES, (c + 1) * 2 * LANES)
            qbd_ref[p, :HD, left] = a
            qbd_ref[p, :HD, right] = zero
            qbd_ref[p, HD:, left] = zero
            qbd_ref[p, HD:, right] = b
    table = views_ref[:count, :].astype(F32).astype(BF16)
    qvis = jnp.dot(table, pick, preferred_element_type=F32).astype(BF16)
    keep = jnp.dot(pick_ref[...].astype(BF16), qvis, preferred_element_type=F32)
    bias = ((keep - 1.0) * BIG).astype(BF16)
    for c in range(chunks):
        part = bias[:, c * LANES : (c + 1) * LANES]
        rows_ref[:, c * 2 * LANES : c * 2 * LANES + LANES] = part
        rows_ref[:, c * 2 * LANES + LANES : (c + 1) * 2 * LANES] = part
    ml_ref[...] = jnp.zeros_like(ml_ref)
    run_tiles((k_ref, v_ref), qbd_ref, rows_ref[:SLOTS, :], (None, None), (acc_ref, ml_ref), (0, PAIRS))


def block_kernel(*refs, step, pieces, pairs, last):
    qbd_ref, rows_ref, acc_in, ml_in = refs[:4]
    kv_refs = refs[4 : 4 + pieces]
    acc_ref, ml_ref = refs[4 + pieces : 6 + pieces]
    rows = rows_ref[step * SLOTS : (step + 1) * SLOTS, :]
    ml_ref[...] = jnp.zeros_like(ml_ref)
    run_tiles(kv_refs, qbd_ref, rows, (acc_in, ml_in), (acc_ref, ml_ref), pairs)
    if last:
        n = pairs[1] - pairs[0]
        send_ref = refs[6 + pieces]
        low = lax.broadcasted_iota(jnp.int32, (HD, LANES), 1) < HD

        def theirs(x, rows):
            a = pltpu.roll(x[:, 2 * LANES : 3 * LANES], HD, 1)
            side = jnp.where(low[:rows], a, x[:, 3 * LANES : 4 * LANES])
            return jnp.concatenate([x[:, 4 * LANES :], side], axis=1)

        for at in range(n):
            send_ref[at * HD : (at + 1) * HD, :] = theirs(acc_ref[at], HD).astype(BF16)
        rest = theirs(jnp.concatenate([ml_ref[:n, :], ml_ref[8 : 8 + n, :]], axis=0), 2 * n)
        parts = []
        for _ in range(3):
            parts.append(rest.astype(BF16).astype(F32))
            rest = rest - parts[-1]
        parts.append(jnp.zeros((packed_rows(n) - n * HD - 6 * n, 3 * LANES), F32))
        send_ref[n * HD :, :] = jnp.concatenate(parts, axis=0).astype(BF16)


def packed_rows(n):
    return n * HD + (6 * n + 15) // 16 * 16


def read_packed(ref, n):
    def spread(x):
        return jnp.concatenate([x, pltpu.roll(x[:, 2 * LANES :], HD, 1)], axis=1)

    tail = ref[n * HD :, :].astype(F32)
    ml = spread(sum(tail[2 * n * i : 2 * n * (i + 1)] for i in range(3)))
    return lambda p: spread(ref[p * HD : (p + 1) * HD, :].astype(F32)), ml[:n], ml[n:]


def last_kernel(
    qbd_ref, rows_ref, acc_in, ml_in, k_ref, kx_ref, v_ref, got_ref, acc_ref, ml_ref, probs_ref, *, step
):
    tok = k_ref.shape[0]
    rows = rows_ref[step * SLOTS : (step + 1) * SLOTS, :]
    marks = key_marks(2 * tok)
    pad = jnp.zeros((LANES - SLOTS, WIDE), BF16)
    ones = jnp.ones((16, tok), BF16)
    got, got_top, got_total = read_packed(got_ref, PAIRS)
    items = [(p, t) for p in range(PAIRS) for t in range(OWN // WIDE)]
    turned, spread = {}, {}

    def score(item):
        p, t = item
        lanes = slice(t * WIDE, (t + 1) * WIDE)
        cols = slice(p * 2 * HD, (p + 1) * 2 * HD)
        keys = jnp.concatenate([k_ref[:, cols], kx_ref[:, cols]], axis=0)
        lhs = jnp.concatenate([keys, marks], axis=1)
        rhs = jnp.concatenate([qbd_ref[p, :, lanes], rows[:, lanes], pad], axis=0)
        return jnp.dot(lhs, rhs, preferred_element_type=F32)

    def soft(item, scores):
        p, t = item
        lanes = slice(t * WIDE, (t + 1) * WIDE)
        old, far = ml_in[p : p + 1, lanes], got_top[p : p + 1, lanes]
        top = jnp.maximum(jnp.max(scores, axis=0, keepdims=True), jnp.maximum(old, far))
        probs = jnp.exp(scores - top).astype(BF16)
        probs_ref[p, :, lanes] = probs[tok:]
        if p not in turned:
            turned[p] = jnp.concatenate([v_ref[:, p * 2 * HD : (p + 1) * 2 * HD].T, ones], axis=0)
            spread[p] = got(p)
        mixed = jnp.dot(turned[p], probs[:tok], preferred_element_type=F32)
        return old, far, top, mixed

    def store(item, old, far, top, mixed):
        p, t = item
        lanes = slice(t * WIDE, (t + 1) * WIDE)
        fa, fb = jnp.exp(old - top), jnp.exp(far - top)
        total = mixed[2 * HD : 2 * HD + 1, :]
        mixed = jnp.concatenate([mixed[:HD, :LANES], mixed[HD : 2 * HD, LANES:]], axis=1)
        acc_ref[p, :, lanes] = mixed + fa * acc_in[p, :, lanes] + fb * spread[p][:, lanes]
        ml_ref[p : p + 1, lanes] = total + fa * ml_in[8 + p : 9 + p, lanes] + fb * got_total[p : p + 1, lanes]

    ml_ref[...] = jnp.zeros_like(ml_ref)
    ready = [score(item) for item in items[:AHEAD]]
    waiting = None
    for i, item in enumerate(items):
        if i + AHEAD < len(items):
            ready.append(score(items[i + AHEAD]))
        now = soft(item, ready.pop(0))
        if waiting is not None:
            store(*waiting)
        waiting = (item, *now)
    store(*waiting)


def finish_kernel(w_ref, acc_ref, ml_ref, probs_ref, v_ref, out_hbm, out_ref, sems):
    tok = out_ref.shape[0]
    ones = jnp.ones((16, tok), BF16)
    parts = []
    for p in range(PAIRS):
        vt = jnp.concatenate([v_ref[:, p * 2 * HD : (p + 1) * 2 * HD].T, ones], axis=0)
        mixed = jnp.dot(vt, probs_ref[p], preferred_element_type=F32)
        share = 1.0 / (ml_ref[p : p + 1, :] + mixed[2 * HD : 2 * HD + 1, :])
        for i in range(2):
            chunks = []
            for t in range(OWN // WIDE):
                lanes = slice(t * WIDE + i * LANES, t * WIDE + (i + 1) * LANES)
                value = acc_ref[p, :, lanes] + mixed[i * HD : (i + 1) * HD, lanes]
                chunks.append((value * share[:, lanes]).astype(BF16))
            parts.append(jnp.concatenate(chunks, axis=1))
    attn = jnp.concatenate(parts, axis=0).T[:tok]
    moves = []
    for c in range(out_ref.shape[1] // CHUNK):
        cols = slice(c * CHUNK, (c + 1) * CHUNK)
        out_ref[:, cols] = jnp.dot(attn, w_ref[:, cols], preferred_element_type=F32).astype(BF16)
        move = pltpu.make_async_copy(out_ref.at[:, cols], out_hbm.at[:, cols], sems.at[c])
        move.start()
        moves.append(move)
    for move in moves:
        move.wait()


def vmem():
    return pl.BlockSpec(memory_space=pltpu.VMEM)


def body(queries, keys, values, out_weight, covis, block_view):
    tok, _ = queries.shape
    count = covis.shape[0]
    n_blk = lax.axis_size("blk")
    half = n_blk // 2
    shape = jax.ShapeDtypeStruct
    swap = [(0, 1), (1, 0)]
    order = ring_order(n_blk)
    ahead = [(order[i], order[(i + 1) % n_blk]) for i in range(n_blk)]
    back = [(b, a) for a, b in ahead]
    params = pltpu.CompilerParams(vmem_limit_bytes=LIMIT)

    def cost(keys_seen, heads):
        return pl.CostEstimate(
            flops=8 * tok * keys_seen * HD * heads,
            bytes_accessed=4 << 20,
            transcendentals=2 * tok * keys_seen * heads,
        )

    other = lax.ppermute(queries, "arc", swap)
    qkv = jnp.concatenate([queries, keys, values], axis=0)
    views = jnp.concatenate([covis, block_view[None]], axis=0)
    qbd, rows, acc, ml = pl.pallas_call(
        functools.partial(first_kernel, n_blk=n_blk),
        out_shape=(
            shape((PAIRS, 2 * HD, 4 * tok), BF16),
            shape(((half + 1) * SLOTS, 4 * tok), BF16),
            shape((PAIRS, HD, 4 * tok), F32),
            shape((16, 4 * tok), F32),
        ),
        in_specs=[vmem()] * 3,
        out_specs=(vmem(),) * 4,
        scratch_shapes=[
            pltpu.SMEM((1, count), jnp.int32),
            pltpu.VMEM(((half + 1) * SLOTS, count), F32),
            pltpu.SemaphoreType.DMA,
        ],
        cost_estimate=cost(tok, HEADS),
        compiler_params=params,
        name="attend_first",
    )(views, qkv, other)

    def attend(acc, ml, pieces, step, pairs=(0, PAIRS), last=False):
        n_pairs = pairs[1] - pairs[0]
        outs = [shape((n_pairs, HD, 4 * tok), F32), shape((16, 4 * tok), F32)]
        if last:
            outs.append(shape((packed_rows(n_pairs), 2 * tok), BF16))
        operands = [qbd, rows, acc, ml, *pieces]
        return pl.pallas_call(
            functools.partial(block_kernel, step=step, pieces=len(pieces), pairs=pairs, last=last),
            out_shape=tuple(outs),
            in_specs=[vmem()] * len(operands),
            out_specs=tuple(vmem() for _ in outs),
            cost_estimate=cost(tok * len(pieces) // 2, 2 * n_pairs),
            compiler_params=params,
            name="attend",
        )(*operands)

    kf = kb = keys
    vf = vb = values
    for step in range(1, half):
        kf = lax.ppermute(kf, "blk", ahead)
        vb = lax.ppermute(vb, "blk", back)
        vf = lax.ppermute(vf, "blk", ahead)
        kb = lax.ppermute(kb, "blk", back)
        got = attend(acc, ml, (kf, vf, kb, vb), step, last=step == half - 1)
        acc, ml = got[:2]
    other = lax.ppermute(got[2], "arc", swap)
    kf = lax.ppermute(kf, "blk", ahead)
    vb = lax.ppermute(vb, "blk", back)
    kx = lax.ppermute(kf, "arc", swap)
    vx = lax.ppermute(vb, "arc", swap)
    finals = pl.pallas_call(
        functools.partial(last_kernel, step=half),
        out_shape=(
            shape((PAIRS, HD, OWN), F32),
            shape((8, OWN), F32),
            shape((PAIRS, tok, OWN), BF16),
        ),
        in_specs=[vmem()] * 8,
        out_specs=(vmem(),) * 3,
        cost_estimate=cost(tok, HEADS),
        compiler_params=params,
        name="close",
    )(qbd, rows, acc, ml, kf, kx, vb, other)
    columns = out_weight.shape[1]
    return pl.pallas_call(
        finish_kernel,
        out_shape=shape((tok, columns), BF16),
        in_specs=[vmem()] * 5,
        out_specs=pl.BlockSpec(memory_space=pl.ANY),
        scratch_shapes=[
            pltpu.VMEM((tok, columns), BF16),
            pltpu.SemaphoreType.DMA((columns // CHUNK,)),
        ],
        compiler_params=params,
        name="finish",
    )(out_weight, *finals, vx)


def solution(mesh):
    return jax.shard_map(
        body,
        mesh=mesh,
        in_specs=(
            P(("groups", "arc", "blk"), None),
            P(("groups", "arc", "blk"), None),
            P(("groups", "arc", "blk"), None),
            P(),
            P("groups", None),
            P("groups"),
        ),
        out_specs=P(("groups", "arc", "blk"), None),
        check_vma=False,
    )
```

```python
import functools

import jax
import jax.numpy as jnp
from jax import lax
from jax.experimental import pallas as pl
from jax.experimental.pallas import tpu as pltpu
from jax.sharding import PartitionSpec as P

HEADS = 10
HD = 64
BLOCK = 32
BIG = 1e30
PAIRS = HEADS // 2
LANES = 128
WIDE = 256
AHEAD = 6
ONES = True
SLOTS = 16
CHUNK = 512
OWN = 512
F32 = jnp.float32
BF16 = jnp.bfloat16
LIMIT = 24 << 20


def ring_order(n):
    if n == 8:
        return [0, 2, 4, 6, 7, 5, 3, 1]
    return list(range(n))


def ring_at(n, place):
    if n == 8:
        return jnp.where(place < 4, 2 * place, 2 * (7 - place) + 1)
    return place


def ring_place(n, blk):
    if n == 8:
        return jnp.where(blk % 2 == 0, blk // 2, 7 - blk // 2)
    return blk


def hops_of(step, n):
    if step == 0:
        return (0,)
    return (step,) if 2 * step == n else (step, n - step)


def query_blocks(tok):
    per = tok // BLOCK
    cut = tok // LANES * LANES // BLOCK
    return [(0, j) for j in range(per)] + [(1, j) for j in range(cut, per)] + [(1, j) for j in range(cut)]


def key_marks(keys, at=0):
    place = lax.broadcasted_iota(jnp.int32, (keys, LANES), 0) // BLOCK
    lane = lax.broadcasted_iota(jnp.int32, (keys, LANES), 1)
    return (place + at == lane).astype(F32).astype(BF16)


def run_tiles(pieces, qbd_ref, rows, state_in, state_out, pairs, at_block=0):
    acc_in, ml_in = state_in
    acc_out, ml_out = state_out
    tok = pieces[0].shape[0]
    parts = len(pieces) // 2
    wide = qbd_ref.shape[2]
    marks = key_marks(parts * tok, at_block)
    pad = jnp.zeros((LANES - SLOTS, WIDE), BF16)
    items = [(at, p, t) for at, p in enumerate(range(*pairs)) for t in range(wide // WIDE)]

    turned = {}
    ones = jnp.ones((16, parts * tok), BF16)

    def joined(refs, p):
        got = [ref[:, p * 2 * HD : (p + 1) * 2 * HD] for ref in refs]
        return got[0] if parts == 1 else jnp.concatenate(got, axis=0)

    def score(item):
        _, p, t = item
        lanes = slice(t * WIDE, (t + 1) * WIDE)
        lhs = jnp.concatenate([joined(pieces[0::2], p), marks], axis=1)
        rhs = jnp.concatenate([qbd_ref[p, :, lanes], rows[:, lanes], pad], axis=0)
        return jnp.dot(lhs, rhs, preferred_element_type=F32)

    def soft(item, scores):
        _, p, t = item
        lanes = slice(t * WIDE, (t + 1) * WIDE)
        top = jnp.max(scores, axis=0, keepdims=True)
        old = None
        if ml_in is not None:
            old = ml_in[p : p + 1, lanes]
            top = jnp.maximum(old, top)
        probs = jnp.exp(scores - top)
        total = None if ONES else jnp.sum(probs, axis=0, keepdims=True)
        if p not in turned:
            turned[p] = joined(pieces[1::2], p).T
            if ONES:
                turned[p] = jnp.concatenate([turned[p], ones], axis=0)
        vt = turned[p]
        mixed = jnp.dot(vt, probs.astype(BF16), preferred_element_type=F32)
        return old, top, total, mixed

    def store(item, old, top, total, mixed):
        at, p, t = item
        lanes = slice(t * WIDE, (t + 1) * WIDE)
        if ONES:
            total = mixed[2 * HD : 2 * HD + 1, :]
        cut = [
            mixed[HD * (i % 2) : HD * (i % 2) + HD, i * LANES : (i + 1) * LANES]
            for i in range(WIDE // LANES)
        ]
        mixed = jnp.concatenate(cut, axis=1)
        if old is not None:
            factor = jnp.exp(old - top)
            total = total + factor * ml_in[8 + p : 9 + p, lanes]
            mixed = mixed + factor * acc_in[p, :, lanes]
        acc_out[at, :, lanes] = mixed
        ml_out[at : at + 1, lanes] = top
        ml_out[8 + at : 9 + at, lanes] = total

    ready = [score(item) for item in items[:AHEAD]]
    waiting = None
    for i, item in enumerate(items):
        if i + AHEAD < len(items):
            ready.append(score(items[i + AHEAD]))
        now = soft(item, ready.pop(0))
        if waiting is not None:
            store(*waiting)
        waiting = (item, *now)
    store(*waiting)


def first_kernel(
    views_ref, qkv_ref, qo_ref, qbd_ref, rows_ref, acc_ref, ml_ref, bv_ref, pick_ref, sem, *, n_blk
):
    tok = qo_ref.shape[0]
    count = views_ref.shape[1]
    q_ref, k_ref, v_ref = (qkv_ref.at[i * tok : (i + 1) * tok] for i in range(3))
    move = pltpu.make_async_copy(views_ref.at[count : count + 1, :], bv_ref, sem)
    move.start()
    per = tok // BLOCK
    cut = tok // LANES * LANES
    chunks = 2 * tok // LANES
    arc = lax.axis_index("arc")
    blk = lax.axis_index("blk")
    place = ring_place(n_blk, blk)
    move.wait()
    lane = lax.broadcasted_iota(jnp.int32, (1, 2 * tok), 1) // BLOCK
    view = jnp.zeros((1, 2 * tok), jnp.int32)
    for at, (half, j) in enumerate(query_blocks(tok)):
        base = ((arc if half == 0 else 1 - arc) * n_blk + blk) * per
        view = jnp.where(lane == at, bv_ref[0, base + j], view)
    sub = lax.broadcasted_iota(jnp.int32, (count, 2 * tok), 0)
    pick = (sub == view).astype(F32).astype(BF16)
    pick_ref[...] = jnp.zeros_like(pick_ref)
    seen = lax.broadcasted_iota(jnp.int32, (1, count), 1)
    for step in range(n_blk // 2 + 1):
        blocks = [(hop, arc) for hop in hops_of(step, n_blk)]
        if 2 * step == n_blk:
            blocks.append((step, 1 - arc))
        for i, (hop, side) in enumerate(blocks):
            far = jnp.where(arc == 0, n_blk - hop, hop)
            base = (side * n_blk + ring_at(n_blk, lax.rem(place + far, n_blk))) * per
            for j in range(per):
                at = step * SLOTS + i * per + j
                pick_ref[at : at + 1, :] = (seen == bv_ref[0, base + j]).astype(F32)
    scale = jnp.asarray(HD ** -0.5, BF16)
    qt = (jnp.concatenate([q_ref[...], qo_ref[cut:, :], qo_ref[:cut, :]], axis=0) * scale).T
    zero = jnp.zeros((HD, LANES), BF16)
    for p in range(PAIRS):
        for c in range(chunks):
            a = qt[p * 2 * HD : p * 2 * HD + HD, c * LANES : (c + 1) * LANES]
            b = qt[p * 2 * HD + HD : (p + 1) * 2 * HD, c * LANES : (c + 1) * LANES]
            left = slice(c * 2 * LANES, c * 2 * LANES + LANES)
            right = slice(c * 2 * LANES + LANES, (c + 1) * 2 * LANES)
            qbd_ref[p, :HD, left] = a
            qbd_ref[p, :HD, right] = zero
            qbd_ref[p, HD:, left] = zero
            qbd_ref[p, HD:, right] = b
    table = views_ref[:count, :].astype(F32).astype(BF16)
    qvis = jnp.dot(table, pick, preferred_element_type=F32).astype(BF16)
    keep = jnp.dot(pick_ref[...].astype(BF16), qvis, preferred_element_type=F32)
    bias = ((keep - 1.0) * BIG).astype(BF16)
    for c in range(chunks):
        part = bias[:, c * LANES : (c + 1) * LANES]
        rows_ref[:, c * 2 * LANES : c * 2 * LANES + LANES] = part
        rows_ref[:, c * 2 * LANES + LANES : (c + 1) * 2 * LANES] = part
    ml_ref[...] = jnp.zeros_like(ml_ref)
    run_tiles((k_ref, v_ref), qbd_ref, rows_ref[:SLOTS, :], (None, None), (acc_ref, ml_ref), (0, PAIRS))


def block_kernel(*refs, step, pieces, pairs, last):
    qbd_ref, rows_ref, acc_in, ml_in = refs[:4]
    kv_refs = refs[4 : 4 + pieces]
    acc_ref, ml_ref = refs[4 + pieces : 6 + pieces]
    rows = rows_ref[step * SLOTS : (step + 1) * SLOTS, :]
    ml_ref[...] = jnp.zeros_like(ml_ref)
    run_tiles(kv_refs, qbd_ref, rows, (acc_in, ml_in), (acc_ref, ml_ref), pairs)
    if last:
        n = pairs[1] - pairs[0]
        send_ref = refs[6 + pieces]
        low = lax.broadcasted_iota(jnp.int32, (HD, LANES), 1) < HD

        def theirs(x, rows):
            a = pltpu.roll(x[:, 2 * LANES : 3 * LANES], HD, 1)
            side = jnp.where(low[:rows], a, x[:, 3 * LANES : 4 * LANES])
            return jnp.concatenate([x[:, 4 * LANES :], side], axis=1)

        for at in range(n):
            send_ref[at * HD : (at + 1) * HD, :] = theirs(acc_ref[at], HD).astype(BF16)
        rest = theirs(jnp.concatenate([ml_ref[:n, :], ml_ref[8 : 8 + n, :]], axis=0), 2 * n)
        parts = []
        for _ in range(3):
            parts.append(rest.astype(BF16).astype(F32))
            rest = rest - parts[-1]
        parts.append(jnp.zeros((packed_rows(n) - n * HD - 6 * n, 3 * LANES), F32))
        send_ref[n * HD :, :] = jnp.concatenate(parts, axis=0).astype(BF16)


def packed_rows(n):
    return n * HD + (6 * n + 15) // 16 * 16


def read_packed(ref, n):
    def spread(x):
        return jnp.concatenate([x, pltpu.roll(x[:, 2 * LANES :], HD, 1)], axis=1)

    tail = ref[n * HD :, :].astype(F32)
    ml = spread(sum(tail[2 * n * i : 2 * n * (i + 1)] for i in range(3)))
    return lambda p: spread(ref[p * HD : (p + 1) * HD, :].astype(F32)), ml[:n], ml[n:]


def last_kernel(qbd_ref, rows_ref, acc_in, ml_in, k_ref, v_ref, got_ref, acc_ref, ml_ref, *, step):
    rows = rows_ref[step * SLOTS : (step + 1) * SLOTS, :OWN]
    ml_ref[...] = jnp.zeros_like(ml_ref)
    own = qbd_ref.at[:, :, :OWN]
    run_tiles((k_ref, v_ref), own, rows, (acc_in, ml_in), (acc_ref, ml_ref), (0, PAIRS))
    got, got_top, got_total = read_packed(got_ref, PAIRS)
    for p in range(PAIRS):
        mine, far = ml_ref[p : p + 1, :], got_top[p : p + 1, :]
        top = jnp.maximum(mine, far)
        fa, fb = jnp.exp(mine - top), jnp.exp(far - top)
        acc_ref[p] = acc_ref[p] * fa + got(p) * fb
        ml_ref[p : p + 1, :] = top
        ml_ref[8 + p : 9 + p, :] = fa * ml_ref[8 + p : 9 + p, :] + fb * got_total[p : p + 1, :]


def finish_kernel(
    w_ref, qbd_ref, rows_ref, acc_in, ml_in, k_ref, v_ref, out_hbm, acc_ref, ml_ref, out_ref, sems, *, step
):
    tok = out_ref.shape[0]
    rows = rows_ref[step * SLOTS : (step + 1) * SLOTS, :OWN]
    own = qbd_ref.at[:, :, :OWN]
    run_tiles(
        (k_ref, v_ref), own, rows, (acc_in, ml_in), (acc_ref, ml_ref), (0, PAIRS), tok // BLOCK
    )
    parts = []
    for p in range(PAIRS):
        share = 1.0 / ml_ref[8 + p : 9 + p, :]
        for i in range(2):
            chunks = []
            for t in range(OWN // WIDE):
                lanes = slice(t * WIDE + i * LANES, t * WIDE + (i + 1) * LANES)
                chunks.append((acc_ref[p, :, lanes] * share[:, lanes]).astype(BF16))
            parts.append(jnp.concatenate(chunks, axis=1))
    attn = jnp.concatenate(parts, axis=0).T[:tok]
    moves = []
    for c in range(out_ref.shape[1] // CHUNK):
        cols = slice(c * CHUNK, (c + 1) * CHUNK)
        out_ref[:, cols] = jnp.dot(attn, w_ref[:, cols], preferred_element_type=F32).astype(BF16)
        move = pltpu.make_async_copy(out_ref.at[:, cols], out_hbm.at[:, cols], sems.at[c])
        move.start()
        moves.append(move)
    for move in moves:
        move.wait()


def vmem():
    return pl.BlockSpec(memory_space=pltpu.VMEM)


def body(queries, keys, values, out_weight, covis, block_view):
    tok, _ = queries.shape
    count = covis.shape[0]
    n_blk = lax.axis_size("blk")
    half = n_blk // 2
    shape = jax.ShapeDtypeStruct
    swap = [(0, 1), (1, 0)]
    order = ring_order(n_blk)
    ring = [(order[i], order[(i + 1) % n_blk]) for i in range(n_blk)]
    ahead = ring + [(n_blk + b, n_blk + a) for a, b in ring]
    back = [(b, a) for a, b in ahead]
    params = pltpu.CompilerParams(vmem_limit_bytes=LIMIT)

    def cost(keys_seen, heads):
        return pl.CostEstimate(
            flops=8 * tok * keys_seen * HD * heads,
            bytes_accessed=4 << 20,
            transcendentals=2 * tok * keys_seen * heads,
        )

    other = lax.ppermute(queries, "arc", swap)
    qkv = jnp.concatenate([queries, keys, values], axis=0)
    views = jnp.concatenate([covis, block_view[None]], axis=0)
    qbd, rows, acc, ml = pl.pallas_call(
        functools.partial(first_kernel, n_blk=n_blk),
        out_shape=(
            shape((PAIRS, 2 * HD, 4 * tok), BF16),
            shape(((half + 1) * SLOTS, 4 * tok), BF16),
            shape((PAIRS, HD, 4 * tok), F32),
            shape((16, 4 * tok), F32),
        ),
        in_specs=[vmem()] * 3,
        out_specs=(vmem(),) * 4,
        scratch_shapes=[
            pltpu.SMEM((1, count), jnp.int32),
            pltpu.VMEM(((half + 1) * SLOTS, count), F32),
            pltpu.SemaphoreType.DMA,
        ],
        cost_estimate=cost(tok, HEADS),
        compiler_params=params,
        name="attend_first",
    )(views, qkv, other)

    def attend(acc, ml, pieces, step, pairs=(0, PAIRS), last=False):
        n_pairs = pairs[1] - pairs[0]
        outs = [shape((n_pairs, HD, 4 * tok), F32), shape((16, 4 * tok), F32)]
        if last:
            outs.append(shape((packed_rows(n_pairs), 2 * tok), BF16))
        operands = [qbd, rows, acc, ml, *pieces]
        return pl.pallas_call(
            functools.partial(block_kernel, step=step, pieces=len(pieces), pairs=pairs, last=last),
            out_shape=tuple(outs),
            in_specs=[vmem()] * len(operands),
            out_specs=tuple(vmem() for _ in outs),
            cost_estimate=cost(tok * len(pieces) // 2, 2 * n_pairs),
            compiler_params=params,
            name="attend",
        )(*operands)

    kf = kb = keys
    vf = vb = values
    for step in range(1, half):
        kf = lax.ppermute(kf, ("arc", "blk"), ahead)
        vb = lax.ppermute(vb, ("arc", "blk"), back)
        vf = lax.ppermute(vf, ("arc", "blk"), ahead)
        kb = lax.ppermute(kb, ("arc", "blk"), back)
        got = attend(acc, ml, (kf, vf, kb, vb), step, last=step == half - 1)
        acc, ml = got[:2]
    other = lax.ppermute(got[2], "arc", swap)
    kf = lax.ppermute(kf, ("arc", "blk"), ahead)
    vb = lax.ppermute(vb, ("arc", "blk"), back)
    kx = lax.ppermute(kf, "arc", swap)
    vx = lax.ppermute(vb, "arc", swap)
    finals = pl.pallas_call(
        functools.partial(last_kernel, step=half),
        out_shape=(shape((PAIRS, HD, OWN), F32), shape((16, OWN), F32)),
        in_specs=[vmem()] * 7,
        out_specs=(vmem(),) * 2,
        cost_estimate=cost(tok, HEADS),
        compiler_params=params,
        name="close",
    )(qbd, rows, acc, ml, kf, vb, other)
    columns = out_weight.shape[1]
    return pl.pallas_call(
        functools.partial(finish_kernel, step=half),
        out_shape=shape((tok, columns), BF16),
        in_specs=[vmem()] * 7,
        out_specs=pl.BlockSpec(memory_space=pl.ANY),
        scratch_shapes=[
            pltpu.VMEM((PAIRS, HD, OWN), F32),
            pltpu.VMEM((16, OWN), F32),
            pltpu.VMEM((tok, columns), BF16),
            pltpu.SemaphoreType.DMA((columns // CHUNK,)),
        ],
        compiler_params=params,
        name="finish",
    )(out_weight, qbd, rows, *finals, kx, vx)


def solution(mesh):
    return jax.shard_map(
        body,
        mesh=mesh,
        in_specs=(
            P(("groups", "arc", "blk"), None),
            P(("groups", "arc", "blk"), None),
            P(("groups", "arc", "blk"), None),
            P(),
            P("groups", None),
            P("groups"),
        ),
        out_specs=P(("groups", "arc", "blk"), None),
        check_vma=False,
    )
```
